512 devices in a mesh: grp: 64 (over x, y, core), swap: 8 (over z).
Axes of the slice: x: 4, y: 8, z: 8, core: 2. Of those that a mesh axis runs over, the one named last changes fastest.
Arguments:
- samples: bfloat16 [8, 64, 64, 4, 4096], P('swap', 'grp'), may hold values from 0.049804688 to 4
- tile_list: int32 [8, 64, 64], replicated, may hold values from 0 to 511, as said below
- tile_slot: int32 [512], replicated, may hold values from 0 to 511, as said below
- brick_rank: int32 [8, 512], replicated, may hold values from 0 to 511, each once within a row
Outputs:
- final_image: float32 [64, 8, 4, 4096], P('grp', None, None, 'swap')
The draws below stay inside these ranges and needn't reach their ends.
Inputs may be any that keep to these rules, and one draw needn't show every extreme that they name: `tile_list`: the 64 tiles of one device are distinct; fragments b * 8 to (b + 1) * 8 - 1 of a device belong to its brick b. With owner(t) = tile_slot[t] // 8, each device has 2 tiles of each of a quarter of the owners of its group, 1 of each of half of them and none of the rest; in every slab one owner has 2 tiles from every device of the group. A permutation: tile t is row tile_slot[t] % 8 of owner tile_slot[t] // 8.
All inputs are finite; a program needn't handle non-finite values.
Results may differ from the reference program's by a relative error of at most 0.0003.
Values sent between devices are 32-bit elements; how exact they have to be, the bound alone decides.
A program may use at most 64 MiB of HBM per device.

```python
import math
import jax
import jax.numpy as jnp
from jax import lax

TILE_PIX = 4096
DEPTH = 4
BRICKS = 8
OWN = 8
FOOT = 64
CAP = 2
SCREEN = 512
N_GRP = 64
N_SWAP = 8


def layout(key):
    base_key = jax.random.fold_in(key, 7)
    tile_slot = jax.random.permutation(jax.random.fold_in(base_key, 1), SCREEN).astype(jnp.int32)
    slot_tile = jnp.argsort(tile_slot).astype(jnp.int32)
    hot_owner = jax.random.randint(jax.random.fold_in(base_key, 2), (N_SWAP,), 0, N_GRP)
    position = jnp.arange(N_GRP, dtype=jnp.int32)
    pattern = jnp.where(position < N_GRP // 4, CAP, jnp.where(position < 3 * N_GRP // 4, CAP // 2, 0))
    scores = jax.random.randint(jax.random.fold_in(base_key, 3), (N_SWAP, N_GRP, N_GRP), 0, 2 ** 20) * N_GRP + position
    scores = jnp.where(position[None, None, :] == hot_owner[:, None, None], -1, scores)
    owner_order = jnp.argsort(scores, axis=-1).astype(jnp.int32)
    within = jnp.arange(OWN, dtype=jnp.int32)
    picked_score = jax.random.randint(jax.random.fold_in(base_key, 4), (N_SWAP, N_GRP, N_GRP, OWN), 0, 2 ** 20) * OWN + within
    picked = jnp.argsort(picked_score, axis=-1)[..., :CAP].astype(jnp.int32)
    chosen = slot_tile[owner_order[..., None] * OWN + picked]
    live_slot = jnp.arange(CAP, dtype=jnp.int32)[None, None, None, :] < pattern[None, None, :, None]
    live_slot = jnp.broadcast_to(live_slot, (N_SWAP, N_GRP, N_GRP, CAP)).reshape(N_SWAP, N_GRP, N_GRP * CAP)
    flat_tiles = chosen.reshape(N_SWAP, N_GRP, N_GRP * CAP)
    rank_key = jnp.where(live_slot, 0, 1) * (N_GRP * CAP) + jnp.arange(N_GRP * CAP, dtype=jnp.int32)
    kept_order = jnp.argsort(rank_key, axis=-1)[..., :FOOT]
    tile_ids = jnp.take_along_axis(flat_tiles, kept_order, axis=-1)
    shuffle_score = jax.random.randint(jax.random.fold_in(base_key, 5), (N_SWAP, N_GRP, FOOT), 0, 2 ** 20) * FOOT + jnp.arange(FOOT, dtype=jnp.int32)
    shuffled = jnp.argsort(shuffle_score, axis=-1)
    tile_ids = jnp.take_along_axis(tile_ids, shuffled, axis=-1)
    return (tile_ids.astype(jnp.int32), tile_slot)


def draw_tile_list(key, part):
    return layout(key)[0]


def draw_tile_slot(key, part):
    return layout(key)[1]


def shard_levels(stream_key, extent, shards, least, top_value):
    gain = 1.0
    for axis_at, parts in shards:
        steps = jax.random.uniform(jax.random.fold_in(jax.random.fold_in(stream_key, 6), axis_at), (parts,), jnp.float32, least / len(shards), top_value / len(shards))
        gain = gain * jnp.repeat(jnp.exp(steps), extent[axis_at] // parts).reshape((-1,) + (1,) * (len(extent) - 1 - axis_at))
    return gain


def setup_inputs(seed: int = 0) -> dict:
    splits = jax.random.split(jax.random.key(seed), 5)
    samples = jnp.clip(jnp.exp(math.log(4.0) - 4.3859405 * jax.random.uniform(splits[0], (N_SWAP, N_GRP, FOOT, DEPTH, TILE_PIX), jnp.float32) ** shard_levels(splits[0], (N_SWAP, N_GRP, FOOT, DEPTH, TILE_PIX), ((0, 8), (1, 64)), -0.2, 0.2)), 0.049804688, 4.0).astype(jnp.bfloat16)
    tile_list = draw_tile_list(jax.random.fold_in(splits[4], 71), 0)
    tile_slot = draw_tile_slot(jax.random.fold_in(splits[4], 71), 0)
    brick_rank = jax.vmap(lambda own: jax.random.permutation(own, N_GRP * BRICKS))(jax.random.split(splits[3], N_SWAP)).reshape((N_SWAP, N_GRP * BRICKS)).astype(jnp.int32)
    return dict(samples=samples, tile_list=tile_list, tile_slot=tile_slot, brick_rank=brick_rank)


EXTINCTION = 0.024


def render(values_in):
    depth_count = values_in.shape[1]
    shape = (values_in.shape[0], values_in.shape[2])
    before = jnp.zeros(shape, jnp.float32)
    red_sum = jnp.zeros(shape, jnp.float32)
    green_sum = jnp.zeros(shape, jnp.float32)
    blue_sum = jnp.zeros(shape, jnp.float32)
    for level in range(depth_count):
        values = values_in[:, level].astype(jnp.float32)
        extinction = EXTINCTION * values
        weight = jnp.exp(-before) * (1.0 - jnp.exp(-extinction))
        ratio = values / (1.0 + values)
        red_sum = red_sum + weight * ratio
        green_sum = green_sum + weight * 4.0 * ratio * (1.0 - ratio)
        blue_sum = blue_sum + weight * (1.0 - ratio)
        before = before + extinction
    return jnp.stack([red_sum, green_sum, blue_sum, before], axis=1)


def reference(samples, tile_list, tile_slot, brick_rank):
    swap_count, group_count, per_device = tile_list.shape
    per_brick = per_device // BRICKS
    flattened = samples.reshape(swap_count * group_count * per_device, DEPTH, TILE_PIX)
    tile_ids = tile_list.reshape(-1).astype(jnp.int32)
    brick_ranks = jnp.repeat(brick_rank.reshape(swap_count, group_count, BRICKS), per_brick, axis=2)
    slab_ids = jnp.arange(swap_count, dtype=jnp.int32)[:, None, None]
    frag_keys = (slab_ids * (group_count * BRICKS) + brick_ranks).reshape(-1).astype(jnp.int32)
    visit_order = jnp.argsort(frag_keys).astype(jnp.int32)
    screen_tiles = tile_slot.shape[0]

    def advance(carry, frag_index):
        colors, optical = carry
        fragment = render(lax.dynamic_slice_in_dim(flattened, frag_index, 1, 0))[0]
        tile_id = tile_ids[frag_index]
        seen_depth = lax.dynamic_index_in_dim(optical, tile_id, 0, keepdims=False)
        old_color = lax.dynamic_index_in_dim(colors, tile_id, 0, keepdims=False)
        colors = lax.dynamic_update_index_in_dim(colors, old_color + jnp.exp(-seen_depth)[None] * fragment[:3], tile_id, 0)
        optical = lax.dynamic_update_index_in_dim(optical, seen_depth + fragment[3], tile_id, 0)
        return (colors, optical), None

    initial = (jnp.zeros((screen_tiles, 3, TILE_PIX), jnp.float32), jnp.zeros((screen_tiles, TILE_PIX), jnp.float32))
    (colors, optical), _ = lax.scan(advance, initial, visit_order)
    slot_tile = jnp.argsort(tile_slot).astype(jnp.int32)
    colors = colors[slot_tile]
    optical = optical[slot_tile]
    final_image = jnp.concatenate([colors, (1.0 - jnp.exp(-optical))[:, None]], axis=1)
    return final_image.reshape(N_GRP, OWN, 4, TILE_PIX)
```

```python
import jax
import jax.numpy as jnp
from jax import lax
from jax.experimental import pallas as pl
from jax.experimental.pallas import tpu as pltpu
from jax.sharding import PartitionSpec as P

BRICKS = 8
LANES = 128
HALF = 64

EXTINCTION = 0.024


def halves(shape):
    return lax.broadcasted_iota(jnp.int32, shape, len(shape) - 1) < HALF


def swapped(value):
    return pltpu.roll(value, HALF, value.ndim - 1)


def render_kernel(samples_ref, out_ref, levels):
    fragments, depth_count, width = samples_ref.shape
    low = halves((fragments, LANES))
    low_half = halves((fragments // 2, LANES))
    for row in range(width // LANES):
        values = samples_ref[:, :, row * LANES : (row + 1) * LANES].astype(jnp.float32)
        levels[...] = values
        passed = jnp.ones((fragments, LANES), jnp.float32)
        red = jnp.zeros((fragments, LANES), jnp.float32)
        green = jnp.zeros((fragments, LANES), jnp.float32)
        for level in range(depth_count):
            value = levels[:, level, :]
            through = jnp.exp(-EXTINCTION * value)
            weight = passed * (1.0 - through)
            rest = 1.0 / (1.0 + value)
            ratio = value * rest
            shade = weight * ratio
            red = red + shade
            green = green + shade * 4.0 * rest
            passed = passed * through
        red_swapped, green_swapped, passed_swapped = swapped(red), swapped(green), swapped(passed)
        half = fragments // 2
        out_ref[2 * row, :fragments, :] = jnp.where(low, red, green_swapped)
        out_ref[2 * row + 1, :fragments, :] = jnp.where(low, red_swapped, green)
        out_ref[2 * row, fragments:, :] = jnp.where(low_half, passed[:half], passed_swapped[half:])
        out_ref[2 * row + 1, fragments:, :] = jnp.where(
            low_half, passed_swapped[:half], passed[half:]
        )


def render(samples, group_count):
    fragments, depth_count, pixels = samples.shape
    steps = 8
    width = pixels // steps
    rows = fragments + fragments // 2
    return pl.pallas_call(
        render_kernel,
        grid=(steps,),
        in_specs=[pl.BlockSpec((fragments, depth_count, width), lambda i: (0, 0, i))],
        out_specs=pl.BlockSpec((group_count // steps, rows, LANES), lambda i: (i, 0, 0)),
        out_shape=jax.ShapeDtypeStruct((group_count, rows, LANES), jnp.float32),
        scratch_shapes=[pltpu.VMEM((fragments, depth_count, LANES), jnp.float32)],
    )(samples)


def composite_kernel(order_ref, slots_ref, pieces_ref, out_ref, through, colors, passed):
    sources, rows, _ = pieces_ref.shape
    fragments = rows * 2 // 3
    half = fragments // 2
    per_brick = fragments // BRICKS
    low_half = halves((half, LANES))

    def widen(source, carry):
        packed = pieces_ref[source, fragments:, :]
        turned = swapped(packed)
        at = pl.multiple_of(source * fragments, fragments)
        through[pl.ds(at, half), :] = jnp.where(low_half, packed, turned)
        through[pl.ds(at + half, half), :] = jnp.where(low_half, turned, packed)
        return carry

    lax.fori_loop(0, sources, widen, 0)
    colors[...] = jnp.zeros_like(colors)
    passed[...] = jnp.ones_like(passed)

    def brick_step(rank, carry):
        brick = order_ref[rank]
        source = brick // BRICKS
        first = (brick % BRICKS) * per_brick
        number = brick * per_brick
        slots = [slots_ref[number + i] for i in range(per_brick)]
        seen = [passed[pl.ds(slot, 1), :] for slot in slots]
        held = [colors[pl.ds(slot, 1), :] for slot in slots]
        shades = [pieces_ref[source, pl.ds(first + i, 1), :] for i in range(per_brick)]
        fades = [through[pl.ds(number + i, 1), :] for i in range(per_brick)]
        for i in range(per_brick):
            colors[pl.ds(slots[i], 1), :] = held[i] + seen[i] * shades[i]
            passed[pl.ds(slots[i], 1), :] = seen[i] * fades[i]
        return carry

    lax.fori_loop(0, order_ref.shape[0], brick_step, 0)
    owned = out_ref.shape[1] // 2
    for owner in range(out_ref.shape[0]):
        out_ref[owner, :owned, :] = colors[owner * owned : (owner + 1) * owned, :]
        out_ref[owner, owned:, :] = passed[owner * owned : (owner + 1) * owned, :]


def composite(pieces, order, slots, owned):
    sources, rows, _ = pieces.shape
    fragments = rows * 2 // 3
    screen = sources * owned
    return pl.pallas_call(
        composite_kernel,
        in_specs=[
            pl.BlockSpec(memory_space=pltpu.SMEM),
            pl.BlockSpec(memory_space=pltpu.SMEM),
            pl.BlockSpec(memory_space=pltpu.VMEM),
        ],
        out_specs=pl.BlockSpec(memory_space=pltpu.VMEM),
        out_shape=jax.ShapeDtypeStruct((sources, 2 * owned, LANES), jnp.float32),
        scratch_shapes=[
            pltpu.VMEM((sources * fragments, LANES), jnp.float32),
            pltpu.VMEM((screen, LANES), jnp.float32),
            pltpu.VMEM((screen, LANES), jnp.float32),
        ],
    )(order, slots, pieces)


def finish_kernel(parts_ref, out_ref):
    slabs, blocks, rows, _ = parts_ref.shape
    owned = rows // 2
    low = halves((owned, LANES))
    for pair in range(blocks // 2):
        ends = []
        for side in range(2):
            block = 2 * pair + side
            color = parts_ref[0, block, :owned, :]
            passed = parts_ref[0, block, owned:, :]
            for slab in range(1, slabs):
                color = color + passed * parts_ref[slab, block, :owned, :]
                passed = passed * parts_ref[slab, block, owned:, :]
            ends.append((color, passed))
        (color_low, passed_low), (color_high, passed_high) = ends
        red = jnp.where(low, color_low, swapped(color_high))
        green = jnp.where(low, swapped(color_low), color_high)
        opacity = 1.0 - jnp.where(low, passed_low, passed_high)
        at = pair * LANES
        out_ref[:, 0, at : at + LANES] = red
        out_ref[:, 1, at : at + LANES] = green
        out_ref[:, 2, at : at + LANES] = opacity - red
        out_ref[:, 3, at : at + LANES] = opacity


def finish(parts):
    slabs, blocks, rows, _ = parts.shape
    return pl.pallas_call(
        finish_kernel,
        out_shape=jax.ShapeDtypeStruct((rows // 2, 4, blocks * HALF), jnp.float32),
    )(parts)


def shards(samples, tile_list, tile_slot, brick_rank):
    group_count = lax.axis_size("grp")
    swap_count = lax.axis_size("swap")
    slab = lax.axis_index("swap")
    screen = tile_slot.shape[0]
    owned = screen // group_count
    pieces = render(samples[0, 0], group_count)
    arrived = lax.all_to_all(pieces, "grp", split_axis=0, concat_axis=0, tiled=True)
    tiles = lax.dynamic_index_in_dim(tile_list, slab, 0, keepdims=False).reshape(-1)
    ranks = lax.dynamic_index_in_dim(brick_rank, slab, 0, keepdims=False)
    number = jnp.arange(screen, dtype=jnp.int32)
    slots = jnp.sum(
        jnp.where(tiles[None, :] == number[:, None], tile_slot[:, None], 0), axis=0, dtype=jnp.int32
    )
    bricks = jnp.arange(ranks.shape[0], dtype=jnp.int32)
    order = jnp.sum(
        jnp.where(ranks[:, None] == bricks[None, :], bricks[:, None], 0), axis=0, dtype=jnp.int32
    )
    partial_image = composite(arrived, order, slots, owned)
    gathered = lax.all_to_all(partial_image, "grp", split_axis=0, concat_axis=0, tiled=True)
    blocks = group_count // swap_count
    parts = lax.all_to_all(
        gathered.reshape(swap_count, blocks, 2 * owned, LANES),
        "swap",
        split_axis=0,
        concat_axis=0,
        tiled=True,
    )
    return finish(parts)[None]


def solution(mesh):
    return jax.shard_map(
        shards,
        mesh=mesh,
        in_specs=(P("swap", "grp", None, None, None), P(), P(), P()),
        out_specs=P("grp", None, None, "swap"),
        check_vma=False,
    )
```

```python
import jax
import jax.numpy as jnp
from jax import lax
from jax.experimental import pallas as pl
from jax.experimental.pallas import tpu as pltpu
from jax.sharding import PartitionSpec as P

BRICKS = 8
LANES = 128
HALF = 64

EXTINCTION = 0.024
MESH = pl.DeviceIdType.MESH


def halves(shape):
    return lax.broadcasted_iota(jnp.int32, shape, len(shape) - 1) < HALF


def swapped(value):
    return pltpu.roll(value, HALF, value.ndim - 1)


def chip_at(step, chips):
    columns = 8 if chips % 32 == 0 else 2
    rows = chips // columns
    mine = lax.axis_index("grp") // 2
    turn = columns - 1 - step // rows
    along = ((turn + 1) // 2) * (2 * (turn % 2) - 1)
    x = (mine // columns + step % rows) % rows
    y = (mine % columns + along + columns) % columns
    return x * columns + y


def render_kernel(samples_ref, out_ref, levels, stage, send_sem, recv_sem, own_sem):
    fragments, depth_count, _ = samples_ref.shape
    group_count = out_ref.shape[0]
    chips = group_count // 2
    half = fragments // 2
    early = chips // 4
    me = lax.axis_index("grp")
    slab = lax.axis_index("swap")
    barrier = pltpu.get_barrier_semaphore()

    def greet(step, carry):
        other = (me + step) % group_count
        pl.semaphore_signal(barrier, inc=1, device_id=(other, slab), device_id_type=MESH)
        return carry

    lax.fori_loop(1, group_count, greet, 0)

    def paint(row):
        at = pl.multiple_of(row * LANES, LANES)
        low = halves((fragments, LANES))
        low_half = halves((half, LANES))
        levels[...] = samples_ref[:, :, pl.ds(at, LANES)].astype(jnp.float32)
        passed = jnp.ones((fragments, LANES), jnp.float32)
        red = jnp.zeros((fragments, LANES), jnp.float32)
        green = jnp.zeros((fragments, LANES), jnp.float32)
        for level in range(depth_count):
            value = levels[:, level, :]
            through = jnp.exp(-EXTINCTION * value)
            weight = passed * (1.0 - through)
            rest = 1.0 / (1.0 + value)
            ratio = value * rest
            shade = weight * ratio
            red = red + shade
            green = green + shade * 4.0 * rest
            passed = passed * through
        red_swapped, green_swapped, passed_swapped = swapped(red), swapped(green), swapped(passed)
        stage[2 * row, :fragments, :] = jnp.where(low, red, green_swapped)
        stage[2 * row + 1, :fragments, :] = jnp.where(low, red_swapped, green)
        stage[2 * row, fragments:, :] = jnp.where(low_half, passed[:half], passed_swapped[half:])
        stage[2 * row + 1, fragments:, :] = jnp.where(
            low_half, passed_swapped[:half], passed[half:]
        )

    def sending(target):
        return pltpu.make_async_remote_copy(
            src_ref=stage.at[target],
            dst_ref=out_ref.at[me],
            send_sem=send_sem.at[target],
            recv_sem=recv_sem.at[me],
            device_id=(target, slab),
            device_id_type=MESH,
        )

    def keeping():
        return pltpu.make_async_copy(stage.at[me], out_ref.at[me], own_sem)

    def send(row):
        for side in range(2):
            target = 2 * row + side

            @pl.when(target != me)
            def _():
                sending(target).start()

            @pl.when(target == me)
            def _():
                keeping().start()

    def first(step, carry):
        paint(chip_at(step, chips))
        return carry

    def first_send(step, carry):
        send(chip_at(step, chips))
        return carry

    def later(step, carry):
        row = chip_at(step, chips)
        paint(row)
        send(row)
        return carry

    lax.fori_loop(0, early, first, 0)
    pl.semaphore_wait(barrier, group_count - 1)
    lax.fori_loop(0, early, first_send, 0)
    lax.fori_loop(early, chips, later, 0)

    def finish_one(step, carry):
        other = (me + step) % group_count
        sending(other).wait_send()
        pltpu.make_async_remote_copy(
            src_ref=stage.at[other],
            dst_ref=out_ref.at[other],
            send_sem=send_sem.at[other],
            recv_sem=recv_sem.at[other],
            device_id=(other, slab),
            device_id_type=MESH,
        ).wait_recv()
        return carry

    lax.fori_loop(1, group_count, finish_one, 0)
    keeping().wait()


def render(samples, group_count):
    fragments, depth_count, pixels = samples.shape
    rows = fragments + fragments // 2
    return pl.pallas_call(
        render_kernel,
        in_specs=[pl.BlockSpec(memory_space=pltpu.VMEM)],
        out_specs=pl.BlockSpec(memory_space=pl.ANY),
        out_shape=jax.ShapeDtypeStruct((group_count, rows, LANES), jnp.float32),
        scratch_shapes=[
            pltpu.VMEM((fragments, depth_count, LANES), jnp.float32),
            pltpu.VMEM((group_count, rows, LANES), jnp.float32),
            pltpu.SemaphoreType.DMA((group_count,)),
            pltpu.SemaphoreType.DMA((group_count,)),
            pltpu.SemaphoreType.DMA,
        ],
        compiler_params=pltpu.CompilerParams(collective_id=0, has_side_effects=True),
        cost_estimate=pl.CostEstimate(
            flops=40 * samples.size, bytes_accessed=8 << 20, transcendentals=samples.size
        ),
    )(samples)


def composite_kernel(order_ref, slots_ref, pieces_ref, out_ref, through, colors, passed):
    sources, rows, _ = pieces_ref.shape
    fragments = rows * 2 // 3
    half = fragments // 2
    per_brick = fragments // BRICKS
    low_half = halves((half, LANES))

    def widen(source, carry):
        packed = pieces_ref[source, fragments:, :]
        turned = swapped(packed)
        at = pl.multiple_of(source * fragments, fragments)
        through[pl.ds(at, half), :] = jnp.where(low_half, packed, turned)
        through[pl.ds(at + half, half), :] = jnp.where(low_half, turned, packed)
        return carry

    lax.fori_loop(0, sources, widen, 0)
    colors[...] = jnp.zeros_like(colors)
    passed[...] = jnp.ones_like(passed)

    def brick_step(rank, carry):
        brick = order_ref[rank]
        source = brick // BRICKS
        first = (brick % BRICKS) * per_brick
        number = brick * per_brick
        slots = [slots_ref[number + i] for i in range(per_brick)]
        seen = [passed[pl.ds(slot, 1), :] for slot in slots]
        held = [colors[pl.ds(slot, 1), :] for slot in slots]
        shades = [pieces_ref[source, pl.ds(first + i, 1), :] for i in range(per_brick)]
        fades = [through[pl.ds(number + i, 1), :] for i in range(per_brick)]
        for i in range(per_brick):
            colors[pl.ds(slots[i], 1), :] = held[i] + seen[i] * shades[i]
            passed[pl.ds(slots[i], 1), :] = seen[i] * fades[i]
        return carry

    lax.fori_loop(0, order_ref.shape[0], brick_step, 0)
    groups, packed_rows, _ = out_ref.shape
    size = packed_rows * 2 // 3
    low_size = halves((size // 2, LANES))
    for group in range(groups):
        at = group * size
        middle = at + size // 2
        out_ref[group, :size, :] = colors[at : at + size, :]
        out_ref[group, size:, :] = jnp.where(
            low_size, passed[at:middle, :], passed[middle : at + size, :]
        )


def composite(pieces, order, slots, screen, groups):
    sources, rows, _ = pieces.shape
    fragments = rows * 2 // 3
    size = screen // groups
    return pl.pallas_call(
        composite_kernel,
        in_specs=[
            pl.BlockSpec(memory_space=pltpu.SMEM),
            pl.BlockSpec(memory_space=pltpu.SMEM),
            pl.BlockSpec(memory_space=pltpu.VMEM),
        ],
        out_specs=pl.BlockSpec(memory_space=pltpu.VMEM),
        out_shape=jax.ShapeDtypeStruct((groups, size + size // 2, LANES), jnp.float32),
        scratch_shapes=[
            pltpu.VMEM((sources * fragments, LANES), jnp.float32),
            pltpu.VMEM((screen, LANES), jnp.float32),
            pltpu.VMEM((screen, LANES), jnp.float32),
        ],
    )(order, slots, pieces)


def finish_kernel(
    part_ref, out_ref, arrived, stage, landed, own_sem, send_sem, recv_sem, out_sem, in_sem, here_sem
):
    slabs, packed_rows, _ = part_ref.shape
    size = packed_rows * 2 // 3
    half = size // 2
    blocks, rows, _ = landed.shape
    owned = rows // 2
    me = lax.axis_index("grp")
    slab = lax.axis_index("swap")
    inside = me // blocks == slab
    barrier = pltpu.get_barrier_semaphore()
    for step in range(1, slabs):
        other = (slab + step) % slabs
        pl.semaphore_signal(barrier, inc=1, device_id=(me, other), device_id_type=MESH)
    for block in range(blocks):
        source = slab * blocks + block

        @pl.when(jnp.logical_not(inside & (source == me)))
        def _():
            pl.semaphore_signal(
                barrier, inc=1, device_id=(source, me // blocks), device_id_type=MESH
            )

    own = pltpu.make_async_copy(part_ref.at[slab], arrived.at[slab], own_sem)
    own.start()

    @pl.when(inside)
    def _():
        pl.semaphore_wait(barrier, slabs + blocks - 2)

    @pl.when(jnp.logical_not(inside))
    def _():
        pl.semaphore_wait(barrier, slabs + blocks - 1)

    def across(other):
        return pltpu.make_async_remote_copy(
            src_ref=part_ref.at[other],
            dst_ref=arrived.at[slab],
            send_sem=send_sem.at[other],
            recv_sem=recv_sem.at[slab],
            device_id=(me, other),
            device_id_type=MESH,
        )

    def from_slab(other):
        return pltpu.make_async_remote_copy(
            src_ref=part_ref.at[other],
            dst_ref=arrived.at[other],
            send_sem=send_sem.at[other],
            recv_sem=recv_sem.at[other],
            device_id=(me, other),
            device_id_type=MESH,
        )

    for step in range(1, slabs):
        across((slab + slabs - step) % slabs).start()
    own.wait()
    low_half = halves((half, LANES))
    color = jnp.zeros((size, LANES), jnp.float32)
    passed = [jnp.ones((half, LANES), jnp.float32)] * 2
    for number in range(slabs):

        @pl.when(slab != number)
        def _():
            from_slab(number).wait_recv()

        packed = arrived[number, size:, :]
        turned = swapped(packed)
        color = color + jnp.concatenate(passed, axis=0) * arrived[number, :size, :]
        passed = [
            passed[0] * jnp.where(low_half, packed, turned),
            passed[1] * jnp.where(low_half, turned, packed),
        ]
    passed = jnp.concatenate(passed, axis=0)

    def to_owner(block):
        return pltpu.make_async_remote_copy(
            src_ref=stage.at[block],
            dst_ref=landed.at[me % blocks],
            send_sem=out_sem.at[block],
            recv_sem=in_sem.at[me % blocks],
            device_id=(slab * blocks + block, me // blocks),
            device_id_type=MESH,
        )

    def from_block(block):
        return pltpu.make_async_remote_copy(
            src_ref=stage.at[block],
            dst_ref=landed.at[block],
            send_sem=out_sem.at[block],
            recv_sem=in_sem.at[block],
            device_id=(slab * blocks + block, me // blocks),
            device_id_type=MESH,
        )

    def stay():
        return pltpu.make_async_copy(stage.at[me % blocks], landed.at[me % blocks], here_sem)

    for block in range(blocks):
        stage[block, :owned, :] = color[block * owned : (block + 1) * owned]
        stage[block, owned:, :] = passed[block * owned : (block + 1) * owned]
    for block in range(blocks):
        here = inside & (slab * blocks + block == me)

        @pl.when(here)
        def _():
            stay().start()

        @pl.when(jnp.logical_not(here))
        def _():
            to_owner(block).start()

    for step in range(1, slabs):
        across((slab + slabs - step) % slabs).wait_send()
    for block in range(blocks):
        here = inside & (slab * blocks + block == me)

        @pl.when(here)
        def _():
            stay().wait()

        @pl.when(jnp.logical_not(here))
        def _():
            to_owner(block).wait_send()
            from_block(block).wait_recv()

    low = halves((owned, LANES))
    for pair in range(blocks // 2):
        color_low, passed_low = landed[2 * pair, :owned, :], landed[2 * pair, owned:, :]
        color_high, passed_high = landed[2 * pair + 1, :owned, :], landed[2 * pair + 1, owned:, :]
        red = jnp.where(low, color_low, swapped(color_high))
        green = jnp.where(low, swapped(color_low), color_high)
        opacity = 1.0 - jnp.where(low, passed_low, passed_high)
        at = pair * LANES
        out_ref[:, 0, at : at + LANES] = red
        out_ref[:, 1, at : at + LANES] = green
        out_ref[:, 2, at : at + LANES] = opacity - red
        out_ref[:, 3, at : at + LANES] = opacity


def finish(parts, group_count, owned):
    slabs = parts.shape[0]
    blocks = group_count // slabs
    return pl.pallas_call(
        finish_kernel,
        in_specs=[pl.BlockSpec(memory_space=pltpu.VMEM)],
        out_specs=pl.BlockSpec(memory_space=pltpu.VMEM),
        out_shape=jax.ShapeDtypeStruct((owned, 4, blocks * HALF), jnp.float32),
        scratch_shapes=[
            pltpu.VMEM(parts.shape, jnp.float32),
            pltpu.VMEM((blocks, 2 * owned, LANES), jnp.float32),
            pltpu.VMEM((blocks, 2 * owned, LANES), jnp.float32),
            pltpu.SemaphoreType.DMA,
            pltpu.SemaphoreType.DMA((slabs,)),
            pltpu.SemaphoreType.DMA((slabs,)),
            pltpu.SemaphoreType.DMA((blocks,)),
            pltpu.SemaphoreType.DMA((blocks,)),
            pltpu.SemaphoreType.DMA,
        ],
        compiler_params=pltpu.CompilerParams(collective_id=1, has_side_effects=True),
    )(parts)


def shards(samples, tile_list, tile_slot, brick_rank):
    group_count = lax.axis_size("grp")
    swap_count = lax.axis_size("swap")
    slab = lax.axis_index("swap")
    screen = tile_slot.shape[0]
    owned = screen // group_count
    arrived = render(samples[0, 0], group_count)
    tiles = lax.dynamic_index_in_dim(tile_list, slab, 0, keepdims=False).reshape(-1)
    ranks = lax.dynamic_index_in_dim(brick_rank, slab, 0, keepdims=False)
    number = jnp.arange(screen, dtype=jnp.int32)
    slots = jnp.sum(
        jnp.where(tiles[None, :] == number[:, None], tile_slot[:, None], 0), axis=0, dtype=jnp.int32
    )
    bricks = jnp.arange(ranks.shape[0], dtype=jnp.int32)
    order = jnp.sum(
        jnp.where(ranks[:, None] == bricks[None, :], bricks[:, None], 0), axis=0, dtype=jnp.int32
    )
    parts = composite(arrived, order, slots, screen, swap_count)
    return finish(parts, group_count, owned)[None]


def solution(mesh):
    return jax.shard_map(
        shards,
        mesh=mesh,
        in_specs=(P("swap", "grp", None, None, None), P(), P(), P()),
        out_specs=P("grp", None, None, "swap"),
        check_vma=False,
    )
```

```python
import functools

import jax
import jax.numpy as jnp
from jax import lax
from jax.experimental import pallas as pl
from jax.experimental.pallas import tpu as pltpu
from jax.sharding import PartitionSpec as P

BRICKS = 8
LANES = 128
HALF = 64

EXTINCTION = 0.024
MESH = pl.DeviceIdType.MESH


def halves(shape):
    return lax.broadcasted_iota(jnp.int32, shape, len(shape) - 1) < HALF


def swapped(value):
    return pltpu.roll(value, HALF, value.ndim - 1)


def chip_at(step, chips):
    columns = 8 if chips % 32 == 0 else 2
    rows = chips // columns
    mine = lax.axis_index("grp") // 2
    turn = columns - 1 - step // rows
    along = ((turn + 1) // 2) * (2 * (turn % 2) - 1)
    x = (mine // columns + step % rows) % rows
    y = (mine % columns + along + columns) % columns
    return x * columns + y


def render_kernel(
    samples_ref,
    tiles_ref,
    tile_slot_ref,
    rank_ref,
    out_ref,
    slots_ref,
    order_ref,
    levels,
    stage,
    send_sem,
    recv_sem,
    own_sem,
):
    fragments, depth_count, _ = samples_ref.shape
    group_count = out_ref.shape[0]
    chips = group_count // 2
    half = fragments // 2
    early = chips // 4
    me = lax.axis_index("grp")
    slab = lax.axis_index("swap")
    barrier = pltpu.get_barrier_semaphore()

    def greet(step, carry):
        other = (me + step) % group_count
        pl.semaphore_signal(barrier, inc=1, device_id=(other, slab), device_id_type=MESH)
        return carry

    lax.fori_loop(1, group_count, greet, 0)

    def paint(row):
        at = pl.multiple_of(row * LANES, LANES)
        low = halves((fragments, LANES))
        low_half = halves((half, LANES))
        levels[...] = samples_ref[:, :, pl.ds(at, LANES)].astype(jnp.float32)
        passed = jnp.ones((fragments, LANES), jnp.float32)
        red = jnp.zeros((fragments, LANES), jnp.float32)
        green = jnp.zeros((fragments, LANES), jnp.float32)
        for level in range(depth_count):
            value = levels[:, level, :]
            through = jnp.exp(-EXTINCTION * value)
            weight = passed * (1.0 - through)
            rest = 1.0 / (1.0 + value)
            ratio = value * rest
            shade = weight * ratio
            red = red + shade
            green = green + shade * 4.0 * rest
            passed = passed * through
        red_swapped, green_swapped, passed_swapped = swapped(red), swapped(green), swapped(passed)
        stage[2 * row, :fragments, :] = jnp.where(low, red, green_swapped)
        stage[2 * row + 1, :fragments, :] = jnp.where(low, red_swapped, green)
        stage[2 * row, fragments:, :] = jnp.where(low_half, passed[:half], passed_swapped[half:])
        stage[2 * row + 1, fragments:, :] = jnp.where(
            low_half, passed_swapped[:half], passed[half:]
        )

    def sending(target):
        return pltpu.make_async_remote_copy(
            src_ref=stage.at[target],
            dst_ref=out_ref.at[me],
            send_sem=send_sem.at[target],
            recv_sem=recv_sem.at[me],
            device_id=(target, slab),
            device_id_type=MESH,
        )

    def keeping():
        return pltpu.make_async_copy(stage.at[me], out_ref.at[me], own_sem)

    def send(row):
        for side in range(2):
            target = 2 * row + side

            @pl.when(target != me)
            def _():
                sending(target).start()

            @pl.when(target == me)
            def _():
                keeping().start()

    def first(step, carry):
        paint(chip_at(step, chips))
        return carry

    def first_send(step, carry):
        send(chip_at(step, chips))
        return carry

    def later(step, carry):
        row = chip_at(step, chips)
        paint(row)
        send(row)
        return carry

    lax.fori_loop(0, early, first, 0)
    pl.semaphore_wait(barrier, group_count - 1)
    lax.fori_loop(0, early, first_send, 0)
    lax.fori_loop(early, chips, later, 0)

    tiles = tiles_ref[slab]

    def find_slot(tile, slots):
        return jnp.where(tiles == tile, tile_slot_ref[tile], slots)

    slots_ref[...] = lax.fori_loop(
        0, tile_slot_ref.shape[0], find_slot, jnp.zeros_like(tiles), unroll=8
    )
    place = lax.broadcasted_iota(jnp.int32, order_ref.shape, 0) * order_ref.shape[1]
    place = place + lax.broadcasted_iota(jnp.int32, order_ref.shape, 1)

    def find_brick(brick, order):
        return jnp.where(place == rank_ref[slab, brick], brick, order)

    order_ref[...] = lax.fori_loop(
        0, rank_ref.shape[1], find_brick, jnp.zeros_like(place), unroll=8
    )

    def finish_one(step, carry):
        other = (me + step) % group_count
        sending(other).wait_send()
        pltpu.make_async_remote_copy(
            src_ref=stage.at[other],
            dst_ref=out_ref.at[other],
            send_sem=send_sem.at[other],
            recv_sem=recv_sem.at[other],
            device_id=(other, slab),
            device_id_type=MESH,
        ).wait_recv()
        return carry

    lax.fori_loop(1, group_count, finish_one, 0)
    keeping().wait()


def render(samples, tile_list, tile_slot, brick_rank, group_count):
    fragments, depth_count, pixels = samples.shape
    rows = fragments + fragments // 2
    bricks = brick_rank.shape[1]
    lanes = min(bricks, LANES)
    return pl.pallas_call(
        render_kernel,
        in_specs=[
            pl.BlockSpec(memory_space=pltpu.VMEM),
            pl.BlockSpec(memory_space=pltpu.VMEM),
            pl.BlockSpec(memory_space=pltpu.SMEM),
            pl.BlockSpec(memory_space=pltpu.SMEM),
        ],
        out_specs=(
            pl.BlockSpec(memory_space=pl.ANY),
            pl.BlockSpec(memory_space=pltpu.VMEM),
            pl.BlockSpec(memory_space=pltpu.VMEM),
        ),
        out_shape=(
            jax.ShapeDtypeStruct((group_count, rows, LANES), jnp.float32),
            jax.ShapeDtypeStruct(tile_list.shape[1:], jnp.int32),
            jax.ShapeDtypeStruct((bricks // lanes, lanes), jnp.int32),
        ),
        scratch_shapes=[
            pltpu.VMEM((fragments, depth_count, LANES), jnp.float32),
            pltpu.VMEM((group_count, rows, LANES), jnp.float32),
            pltpu.SemaphoreType.DMA((group_count,)),
            pltpu.SemaphoreType.DMA((group_count,)),
            pltpu.SemaphoreType.DMA,
        ],
        compiler_params=pltpu.CompilerParams(collective_id=0, has_side_effects=True),
        cost_estimate=pl.CostEstimate(
            flops=40 * samples.size, bytes_accessed=8 << 20, transcendentals=samples.size
        ),
    )(samples, tile_list, tile_slot, brick_rank)


def composite_kernel(
    order_ref, slots_ref, pieces_ref, out_ref, through, colors, passed, *, fragments
):
    rows = fragments * 3 // 2
    sources = pieces_ref.shape[0] // rows
    half = fragments // 2
    per_brick = fragments // BRICKS
    bricks = sources * BRICKS
    clear = colors.shape[0] // sources
    low_half = halves((half, LANES))

    def widen(source, carry):
        start = pl.multiple_of(source * rows + fragments, 8)
        packed = pieces_ref[pl.ds(start, half), :]
        turned = swapped(packed)
        at = pl.multiple_of(source * fragments, fragments)
        through[pl.ds(at, half), :] = jnp.where(low_half, packed, turned)
        through[pl.ds(at + half, half), :] = jnp.where(low_half, turned, packed)
        empty = pl.multiple_of(source * clear, clear)
        colors[pl.ds(empty, clear), :] = jnp.zeros((clear, LANES), jnp.float32)
        passed[pl.ds(empty, clear), :] = jnp.ones((clear, LANES), jnp.float32)
        return carry

    lax.fori_loop(0, sources, widen, 0)

    def fetch(brick):
        return tuple(slots_ref[brick * per_brick + i] for i in range(per_brick))

    def brick_step(rank, carry):
        brick, after, slots = carry
        later = order_ref[jnp.minimum(rank + 2, bricks - 1)]
        slots_after = fetch(after)
        source = jnp.right_shift(brick, BRICKS.bit_length() - 1)
        first = source * rows + (brick & (BRICKS - 1)) * per_brick
        number = brick * per_brick
        seen = [passed[pl.ds(slot, 1), :] for slot in slots]
        held = [colors[pl.ds(slot, 1), :] for slot in slots]
        shades = [pieces_ref[pl.ds(first + i, 1), :] for i in range(per_brick)]
        fades = [through[pl.ds(number + i, 1), :] for i in range(per_brick)]
        for i in range(per_brick):
            passed[pl.ds(slots[i], 1), :] = seen[i] * fades[i]
            colors[pl.ds(slots[i], 1), :] = held[i] + seen[i] * shades[i]
        return after, later, slots_after

    first_brick = order_ref[0]
    lax.fori_loop(
        0, bricks, brick_step, (first_brick, order_ref[1], fetch(first_brick)), unroll=2
    )
    groups, packed_rows, _ = out_ref.shape
    size = packed_rows * 2 // 3
    low_size = halves((size // 2, LANES))
    for group in range(groups):
        at = group * size
        middle = at + size // 2
        out_ref[group, :size, :] = colors[at : at + size, :]
        out_ref[group, size:, :] = jnp.where(
            low_size, passed[at:middle, :], passed[middle : at + size, :]
        )


def composite(pieces, order, slots, screen, groups):
    sources, rows, _ = pieces.shape
    fragments = rows * 2 // 3
    size = screen // groups
    return pl.pallas_call(
        functools.partial(composite_kernel, fragments=fragments),
        in_specs=[
            pl.BlockSpec(memory_space=pltpu.SMEM),
            pl.BlockSpec(memory_space=pltpu.SMEM),
            pl.BlockSpec(memory_space=pltpu.VMEM),
        ],
        out_specs=pl.BlockSpec(memory_space=pltpu.VMEM),
        out_shape=jax.ShapeDtypeStruct((groups, size + size // 2, LANES), jnp.float32),
        scratch_shapes=[
            pltpu.VMEM((sources * fragments, LANES), jnp.float32),
            pltpu.VMEM((screen, LANES), jnp.float32),
            pltpu.VMEM((screen, LANES), jnp.float32),
        ],
    )(order, slots, pieces.reshape(sources * rows, LANES))


def finish_kernel(
    part_ref, out_ref, arrived, stage, landed, own_sem, send_sem, recv_sem, out_sem, in_sem, here_sem
):
    slabs, packed_rows, _ = part_ref.shape
    size = packed_rows * 2 // 3
    half = size // 2
    blocks, rows, _ = landed.shape
    owned = rows // 2
    me = lax.axis_index("grp")
    slab = lax.axis_index("swap")
    inside = me // blocks == slab
    barrier = pltpu.get_barrier_semaphore()
    for step in range(1, slabs):
        other = (slab + step) % slabs
        pl.semaphore_signal(barrier, inc=1, device_id=(me, other), device_id_type=MESH)
    for block in range(blocks):
        source = slab * blocks + block

        @pl.when(jnp.logical_not(inside & (source == me)))
        def _():
            pl.semaphore_signal(
                barrier, inc=1, device_id=(source, me // blocks), device_id_type=MESH
            )

    own = pltpu.make_async_copy(part_ref.at[slab], arrived.at[slab], own_sem)
    own.start()

    @pl.when(inside)
    def _():
        pl.semaphore_wait(barrier, slabs + blocks - 2)

    @pl.when(jnp.logical_not(inside))
    def _():
        pl.semaphore_wait(barrier, slabs + blocks - 1)

    def across(other):
        return pltpu.make_async_remote_copy(
            src_ref=part_ref.at[other],
            dst_ref=arrived.at[slab],
            send_sem=send_sem.at[other],
            recv_sem=recv_sem.at[slab],
            device_id=(me, other),
            device_id_type=MESH,
        )

    def from_slab(other):
        return pltpu.make_async_remote_copy(
            src_ref=part_ref.at[other],
            dst_ref=arrived.at[other],
            send_sem=send_sem.at[other],
            recv_sem=recv_sem.at[other],
            device_id=(me, other),
            device_id_type=MESH,
        )

    for step in range(1, slabs):
        across((slab + slabs - step) % slabs).start()
    own.wait()
    low_half = halves((half, LANES))
    color = jnp.zeros((size, LANES), jnp.float32)
    passed = [jnp.ones((half, LANES), jnp.float32)] * 2
    for number in range(slabs):

        @pl.when(slab != number)
        def _():
            from_slab(number).wait_recv()

        packed = arrived[number, size:, :]
        turned = swapped(packed)
        color = color + jnp.concatenate(passed, axis=0) * arrived[number, :size, :]
        passed = [
            passed[0] * jnp.where(low_half, packed, turned),
            passed[1] * jnp.where(low_half, turned, packed),
        ]
    passed = jnp.concatenate(passed, axis=0)

    def to_owner(block):
        return pltpu.make_async_remote_copy(
            src_ref=stage.at[block],
            dst_ref=landed.at[me % blocks],
            send_sem=out_sem.at[block],
            recv_sem=in_sem.at[me % blocks],
            device_id=(slab * blocks + block, me // blocks),
            device_id_type=MESH,
        )

    def from_block(block):
        return pltpu.make_async_remote_copy(
            src_ref=stage.at[block],
            dst_ref=landed.at[block],
            send_sem=out_sem.at[block],
            recv_sem=in_sem.at[block],
            device_id=(slab * blocks + block, me // blocks),
            device_id_type=MESH,
        )

    def stay():
        return pltpu.make_async_copy(stage.at[me % blocks], landed.at[me % blocks], here_sem)

    for block in range(blocks):
        stage[block, :owned, :] = color[block * owned : (block + 1) * owned]
        stage[block, owned:, :] = passed[block * owned : (block + 1) * owned]
    for block in range(blocks):
        here = inside & (slab * blocks + block == me)

        @pl.when(here)
        def _():
            stay().start()

        @pl.when(jnp.logical_not(here))
        def _():
            to_owner(block).start()

    for step in range(1, slabs):
        across((slab + slabs - step) % slabs).wait_send()
    for block in range(blocks):
        here = inside & (slab * blocks + block == me)

        @pl.when(here)
        def _():
            stay().wait()

        @pl.when(jnp.logical_not(here))
        def _():
            to_owner(block).wait_send()
            from_block(block).wait_recv()

    low = halves((owned, LANES))
    for pair in range(blocks // 2):
        color_low, passed_low = landed[2 * pair, :owned, :], landed[2 * pair, owned:, :]
        color_high, passed_high = landed[2 * pair + 1, :owned, :], landed[2 * pair + 1, owned:, :]
        red = jnp.where(low, color_low, swapped(color_high))
        green = jnp.where(low, swapped(color_low), color_high)
        opacity = 1.0 - jnp.where(low, passed_low, passed_high)
        at = pair * LANES
        out_ref[:, 0, at : at + LANES] = red
        out_ref[:, 1, at : at + LANES] = green
        out_ref[:, 2, at : at + LANES] = opacity - red
        out_ref[:, 3, at : at + LANES] = opacity


def finish(parts, group_count, owned):
    slabs = parts.shape[0]
    blocks = group_count // slabs
    return pl.pallas_call(
        finish_kernel,
        in_specs=[pl.BlockSpec(memory_space=pltpu.VMEM)],
        out_specs=pl.BlockSpec(memory_space=pltpu.VMEM),
        out_shape=jax.ShapeDtypeStruct((owned, 4, blocks * HALF), jnp.float32),
        scratch_shapes=[
            pltpu.VMEM(parts.shape, jnp.float32),
            pltpu.VMEM((blocks, 2 * owned, LANES), jnp.float32),
            pltpu.VMEM((blocks, 2 * owned, LANES), jnp.float32),
            pltpu.SemaphoreType.DMA,
            pltpu.SemaphoreType.DMA((slabs,)),
            pltpu.SemaphoreType.DMA((slabs,)),
            pltpu.SemaphoreType.DMA((blocks,)),
            pltpu.SemaphoreType.DMA((blocks,)),
            pltpu.SemaphoreType.DMA,
        ],
        compiler_params=pltpu.CompilerParams(collective_id=1, has_side_effects=True),
    )(parts)


def shards(samples, tile_list, tile_slot, brick_rank):
    group_count = lax.axis_size("grp")
    swap_count = lax.axis_size("swap")
    screen = tile_slot.shape[0]
    owned = screen // group_count
    arrived, slots, order = render(samples[0, 0], tile_list, tile_slot, brick_rank, group_count)
    parts = composite(arrived, order.reshape(-1), slots.reshape(-1), screen, swap_count)
    return finish(parts, group_count, owned)[None]


def solution(mesh):
    return jax.shard_map(
        shards,
        mesh=mesh,
        in_specs=(P("swap", "grp", None, None, None), P(), P(), P()),
        out_specs=P("grp", None, None, "swap"),
        check_vma=False,
    )
```

```python
import functools

import jax
import jax.numpy as jnp
from jax import lax
from jax.experimental import pallas as pl
from jax.experimental.pallas import tpu as pltpu
from jax.sharding import PartitionSpec as P

BRICKS = 8
LANES = 128
HALF = 64

EXTINCTION = 0.024
MESH = pl.DeviceIdType.MESH


def halves(shape):
    return lax.broadcasted_iota(jnp.int32, shape, len(shape) - 1) < HALF


def swapped(value):
    return pltpu.roll(value, HALF, value.ndim - 1)


def chip_at(step, chips):
    columns = 8 if chips % 32 == 0 else 2
    rows = chips // columns
    mine = lax.axis_index("grp") // 2
    turn = columns - 1 - step // rows
    along = ((turn + 1) // 2) * (2 * (turn % 2) - 1)
    x = (mine // columns + step % rows) % rows
    y = (mine % columns + along + columns) % columns
    return x * columns + y


def render_kernel(
    samples_ref,
    tiles_ref,
    tile_slot_ref,
    rank_ref,
    out_ref,
    slots_ref,
    order_ref,
    start_ref,
    levels,
    stage,
    send_sem,
    recv_sem,
    own_sem,
):
    fragments, depth_count, _ = samples_ref.shape
    group_count = out_ref.shape[0]
    chips = group_count // 2
    half = fragments // 2
    early = chips // 8 if chips % 8 == 0 else 1
    me = lax.axis_index("grp")
    slab = lax.axis_index("swap")
    barrier = pltpu.get_barrier_semaphore()

    def greet(step, carry):
        other = (me + step) % group_count
        pl.semaphore_signal(barrier, inc=1, device_id=(other, slab), device_id_type=MESH)
        return carry

    lax.fori_loop(1, group_count, greet, 0)

    def paint(row):
        at = pl.multiple_of(row * LANES, LANES)
        low = halves((fragments, LANES))
        low_half = halves((half, LANES))
        levels[...] = samples_ref[:, :, pl.ds(at, LANES)].astype(jnp.float32)
        passed = jnp.ones((fragments, LANES), jnp.float32)
        red = jnp.zeros((fragments, LANES), jnp.float32)
        green = jnp.zeros((fragments, LANES), jnp.float32)
        for level in range(depth_count):
            value = levels[:, level, :]
            through = jnp.exp(-EXTINCTION * value)
            weight = passed * (1.0 - through)
            rest = 1.0 / (1.0 + value)
            ratio = value * rest
            shade = weight * ratio
            red = red + shade
            green = green + shade * 4.0 * rest
            passed = passed * through
        red_swapped, green_swapped, passed_swapped = swapped(red), swapped(green), swapped(passed)
        stage[2 * row, :fragments, :] = jnp.where(low, red, green_swapped)
        stage[2 * row + 1, :fragments, :] = jnp.where(low, red_swapped, green)
        stage[2 * row, fragments:, :] = jnp.where(low_half, passed[:half], passed_swapped[half:])
        stage[2 * row + 1, fragments:, :] = jnp.where(
            low_half, passed_swapped[:half], passed[half:]
        )

    def sending(target):
        return pltpu.make_async_remote_copy(
            src_ref=stage.at[target],
            dst_ref=out_ref.at[me],
            send_sem=send_sem.at[target],
            recv_sem=recv_sem.at[me],
            device_id=(target, slab),
            device_id_type=MESH,
        )

    def keeping():
        return pltpu.make_async_copy(stage.at[me], out_ref.at[me], own_sem)

    def send(row):
        for side in range(2):
            target = 2 * row + side

            @pl.when(target != me)
            def _():
                sending(target).start()

            @pl.when(target == me)
            def _():
                keeping().start()

    def first(step, carry):
        paint(chip_at(step, chips))
        return carry

    def first_send(step, carry):
        send(chip_at(step, chips))
        return carry

    def later(step, carry):
        row = chip_at(step, chips)
        paint(row)
        send(row)
        return carry

    lax.fori_loop(0, early, first, 0)
    pl.semaphore_wait(barrier, group_count - 1)
    lax.fori_loop(0, early, first_send, 0)
    lax.fori_loop(early, chips, later, 0)

    tiles = tiles_ref[slab]

    def find_slot(tile, slots):
        return jnp.where(tiles == tile, 2 * tile_slot_ref[tile], slots)

    slots = lax.fori_loop(
        0, tile_slot_ref.shape[0], find_slot, jnp.zeros_like(tiles), unroll=8
    )
    pairs = group_count // 2
    slots_ref[...] = jnp.concatenate([slots[:pairs], slots[pairs:]], axis=1)
    place = lax.broadcasted_iota(jnp.int32, order_ref.shape, 0) * order_ref.shape[1]
    place = place + lax.broadcasted_iota(jnp.int32, order_ref.shape, 1)

    def find_brick(brick, order):
        return jnp.where(place == rank_ref[slab, brick], brick, order)

    order = lax.fori_loop(0, rank_ref.shape[1], find_brick, jnp.zeros_like(place), unroll=8)
    per_brick = fragments // BRICKS
    source = order // BRICKS
    upper = (source >= pairs).astype(jnp.int32)
    order_ref[...] = order * (2 * per_brick)
    start_ref[...] = (
        (source - upper * pairs) * (2 * fragments)
        + upper * fragments
        + (order - source * BRICKS) * per_brick
    )

    def finish_one(step, carry):
        other = (me + step) % group_count
        sending(other).wait_send()
        pltpu.make_async_remote_copy(
            src_ref=stage.at[other],
            dst_ref=out_ref.at[other],
            send_sem=send_sem.at[other],
            recv_sem=recv_sem.at[other],
            device_id=(other, slab),
            device_id_type=MESH,
        ).wait_recv()
        return carry

    lax.fori_loop(1, group_count, finish_one, 0)
    keeping().wait()


def render(samples, tile_list, tile_slot, brick_rank, group_count):
    fragments, depth_count, pixels = samples.shape
    rows = fragments + fragments // 2
    bricks = brick_rank.shape[1]
    lanes = min(bricks, LANES)
    return pl.pallas_call(
        render_kernel,
        in_specs=[
            pl.BlockSpec(memory_space=pltpu.VMEM),
            pl.BlockSpec(memory_space=pltpu.VMEM),
            pl.BlockSpec(memory_space=pltpu.SMEM),
            pl.BlockSpec(memory_space=pltpu.SMEM),
        ],
        out_specs=(
            pl.BlockSpec(memory_space=pl.ANY),
            pl.BlockSpec(memory_space=pltpu.VMEM),
            pl.BlockSpec(memory_space=pltpu.VMEM),
            pl.BlockSpec(memory_space=pltpu.VMEM),
        ),
        out_shape=(
            jax.ShapeDtypeStruct((group_count, rows, LANES), jnp.float32),
            jax.ShapeDtypeStruct((group_count // 2, 2 * fragments), jnp.int32),
            jax.ShapeDtypeStruct((bricks // lanes, lanes), jnp.int32),
            jax.ShapeDtypeStruct((bricks // lanes, lanes), jnp.int32),
        ),
        scratch_shapes=[
            pltpu.VMEM((fragments, depth_count, LANES), jnp.float32),
            pltpu.VMEM((group_count, rows, LANES), jnp.float32),
            pltpu.SemaphoreType.DMA((group_count,)),
            pltpu.SemaphoreType.DMA((group_count,)),
            pltpu.SemaphoreType.DMA,
        ],
        compiler_params=pltpu.CompilerParams(collective_id=0, has_side_effects=True),
        cost_estimate=pl.CostEstimate(
            flops=40 * samples.size, bytes_accessed=8 << 20, transcendentals=samples.size
        ),
    )(samples, tile_list, tile_slot, brick_rank)


def composite_kernel(
    order_ref, start_ref, slots_ref, pieces_ref, out_ref, parts, state, *, fragments
):
    rows = fragments * 3 // 2
    sources = pieces_ref.shape[0] // rows
    half = fragments // 2
    per_brick = fragments // BRICKS
    bricks = sources * BRICKS
    clear = state.shape[0] // sources
    low_half = halves((half, LANES))
    odd = lax.broadcasted_iota(jnp.int32, (clear, LANES), 0) & 1
    upper = lax.broadcasted_iota(jnp.int32, (2, LANES), 0) == 0

    def widen(source, carry):
        start = pl.multiple_of(source * rows, 8)
        packed = pieces_ref[pl.ds(start + fragments, half), :]
        turned = swapped(packed)
        at = pl.multiple_of(source * (2 * fragments), 8)
        parts[pl.ds(at, fragments, stride=2), :] = pieces_ref[pl.ds(start, fragments), :]
        parts[pl.ds(at + 1, half, stride=2), :] = jnp.where(low_half, packed, turned)
        parts[pl.ds(at + fragments + 1, half, stride=2), :] = jnp.where(low_half, turned, packed)
        state[pl.ds(pl.multiple_of(source * clear, clear), clear), :] = odd.astype(jnp.float32)
        return carry

    lax.fori_loop(0, sources, widen, 0)

    def fetch(start):
        return tuple(slots_ref[start + i] for i in range(per_brick))

    def brick_step(rank, slots):
        slots_after = fetch(start_ref[jnp.minimum(rank + 1, bricks - 1)])
        at = pl.multiple_of(order_ref[rank], 2 * per_brick)
        held = [state[pl.ds(pl.multiple_of(slot, 2), 2), :] for slot in slots]
        for i in range(per_brick):
            seen = jnp.broadcast_to(held[i][1:], (2, LANES))
            added = seen * parts[pl.ds(at + 2 * i, 2), :]
            state[pl.ds(pl.multiple_of(slots[i], 2), 2), :] = added + jnp.where(
                upper, held[i], 0.0
            )
        return slots_after

    lax.fori_loop(0, bricks, brick_step, fetch(start_ref[0]), unroll=2)
    groups, packed_rows, _ = out_ref.shape
    size = packed_rows * 2 // 3
    low_size = halves((size // 2, LANES))
    for group in range(groups):
        at = group * 2 * size
        out_ref[group, :size, :] = state[pl.ds(at, size, stride=2), :]
        out_ref[group, size:, :] = jnp.where(
            low_size,
            state[pl.ds(at + 1, size // 2, stride=2), :],
            state[pl.ds(at + size + 1, size // 2, stride=2), :],
        )


def composite(pieces, order, start, slots, screen, groups):
    sources, rows, _ = pieces.shape
    fragments = rows * 2 // 3
    size = screen // groups
    return pl.pallas_call(
        functools.partial(composite_kernel, fragments=fragments),
        in_specs=[
            pl.BlockSpec(memory_space=pltpu.SMEM),
            pl.BlockSpec(memory_space=pltpu.SMEM),
            pl.BlockSpec(memory_space=pltpu.SMEM),
            pl.BlockSpec(memory_space=pltpu.VMEM),
        ],
        out_specs=pl.BlockSpec(memory_space=pltpu.VMEM),
        out_shape=jax.ShapeDtypeStruct((groups, size + size // 2, LANES), jnp.float32),
        scratch_shapes=[
            pltpu.VMEM((2 * sources * fragments, LANES), jnp.float32),
            pltpu.VMEM((2 * screen, LANES), jnp.float32),
        ],
    )(order, start, slots, pieces.reshape(sources * rows, LANES))


def finish_kernel(
    part_ref, out_ref, arrived, stage, landed, own_sem, send_sem, recv_sem, out_sem, in_sem, here_sem
):
    packed_rows = part_ref.shape[1]
    slabs = part_ref.shape[0] // 2
    size = packed_rows * 2 // 3
    half = size // 2
    blocks, rows, _ = landed.shape
    owned = rows // 2
    me = lax.axis_index("grp")
    slab = lax.axis_index("swap")
    inside = me // blocks == slab
    barrier = pltpu.get_barrier_semaphore()
    for step in range(1, slabs):
        other = (slab + step) % slabs
        pl.semaphore_signal(barrier, inc=1, device_id=(me, other), device_id_type=MESH)
    for block in range(blocks):
        source = slab * blocks + block

        @pl.when(jnp.logical_not(inside & (source == me)))
        def _():
            pl.semaphore_signal(
                barrier, inc=1, device_id=(source, me // blocks), device_id_type=MESH
            )

    def own(side):
        return pltpu.make_async_copy(
            part_ref.at[2 * slab + side], arrived.at[side, slab], own_sem.at[side]
        )

    own(0).start()
    own(1).start()

    @pl.when(inside)
    def _():
        pl.semaphore_wait(barrier, slabs + blocks - 2)

    @pl.when(jnp.logical_not(inside))
    def _():
        pl.semaphore_wait(barrier, slabs + blocks - 1)

    def across(side, other):
        return pltpu.make_async_remote_copy(
            src_ref=part_ref.at[2 * other + side],
            dst_ref=arrived.at[side, slab],
            send_sem=send_sem.at[side, other],
            recv_sem=recv_sem.at[side, slab],
            device_id=(me, other),
            device_id_type=MESH,
        )

    def from_slab(side, other):
        return pltpu.make_async_remote_copy(
            src_ref=part_ref.at[2 * other + side],
            dst_ref=arrived.at[side, other],
            send_sem=send_sem.at[side, other],
            recv_sem=recv_sem.at[side, other],
            device_id=(me, other),
            device_id_type=MESH,
        )

    for side in range(2):
        for step in range(1, slabs):
            across(side, (slab + slabs - step) % slabs).start()
    low_half = halves((half, LANES))

    def merge(side):
        own(side).wait()
        color = jnp.zeros((size, LANES), jnp.float32)
        passed = [jnp.ones((half, LANES), jnp.float32)] * 2
        for number in range(slabs):

            @pl.when(slab != number)
            def _():
                from_slab(side, number).wait_recv()

            packed = arrived[side, number, size:, :]
            turned = swapped(packed)
            color = color + jnp.concatenate(passed, axis=0) * arrived[side, number, :size, :]
            passed = [
                passed[0] * jnp.where(low_half, packed, turned),
                passed[1] * jnp.where(low_half, turned, packed),
            ]
        return color, jnp.concatenate(passed, axis=0)

    def to_owner(block):
        return pltpu.make_async_remote_copy(
            src_ref=stage.at[block],
            dst_ref=landed.at[me % blocks],
            send_sem=out_sem.at[block],
            recv_sem=in_sem.at[me % blocks],
            device_id=(slab * blocks + block, me // blocks),
            device_id_type=MESH,
        )

    def from_block(block):
        return pltpu.make_async_remote_copy(
            src_ref=stage.at[block],
            dst_ref=landed.at[block],
            send_sem=out_sem.at[block],
            recv_sem=in_sem.at[block],
            device_id=(slab * blocks + block, me // blocks),
            device_id_type=MESH,
        )

    def stay():
        return pltpu.make_async_copy(stage.at[me % blocks], landed.at[me % blocks], here_sem)

    for side in range(2):
        color, passed = merge(side)
        first = side * blocks // 2
        for block in range(first, first + blocks // 2):
            at = (block - first) * owned
            stage[block, :owned, :] = color[at : at + owned]
            stage[block, owned:, :] = passed[at : at + owned]
        for block in range(first, first + blocks // 2):
            here = inside & (slab * blocks + block == me)

            @pl.when(here)
            def _():
                stay().start()

            @pl.when(jnp.logical_not(here))
            def _():
                to_owner(block).start()

    for side in range(2):
        for step in range(1, slabs):
            across(side, (slab + slabs - step) % slabs).wait_send()
    for block in range(blocks):
        here = inside & (slab * blocks + block == me)

        @pl.when(here)
        def _():
            stay().wait()

        @pl.when(jnp.logical_not(here))
        def _():
            to_owner(block).wait_send()
            from_block(block).wait_recv()

    low = halves((owned, LANES))
    for pair in range(blocks // 2):
        color_low, passed_low = landed[2 * pair, :owned, :], landed[2 * pair, owned:, :]
        color_high, passed_high = landed[2 * pair + 1, :owned, :], landed[2 * pair + 1, owned:, :]
        red = jnp.where(low, color_low, swapped(color_high))
        green = jnp.where(low, swapped(color_low), color_high)
        opacity = 1.0 - jnp.where(low, passed_low, passed_high)
        at = pair * LANES
        out_ref[:, 0, at : at + LANES] = red
        out_ref[:, 1, at : at + LANES] = green
        out_ref[:, 2, at : at + LANES] = opacity - red
        out_ref[:, 3, at : at + LANES] = opacity


def finish(parts, slabs, group_count, owned):
    blocks = group_count // slabs
    return pl.pallas_call(
        finish_kernel,
        in_specs=[pl.BlockSpec(memory_space=pltpu.VMEM)],
        out_specs=pl.BlockSpec(memory_space=pltpu.VMEM),
        out_shape=jax.ShapeDtypeStruct((owned, 4, blocks * HALF), jnp.float32),
        scratch_shapes=[
            pltpu.VMEM((2, slabs) + parts.shape[1:], jnp.float32),
            pltpu.VMEM((blocks, 2 * owned, LANES), jnp.float32),
            pltpu.VMEM((blocks, 2 * owned, LANES), jnp.float32),
            pltpu.SemaphoreType.DMA((2,)),
            pltpu.SemaphoreType.DMA((2, slabs)),
            pltpu.SemaphoreType.DMA((2, slabs)),
            pltpu.SemaphoreType.DMA((blocks,)),
            pltpu.SemaphoreType.DMA((blocks,)),
            pltpu.SemaphoreType.DMA,
        ],
        compiler_params=pltpu.CompilerParams(collective_id=1, has_side_effects=True),
    )(parts)


def shards(samples, tile_list, tile_slot, brick_rank):
    group_count = lax.axis_size("grp")
    swap_count = lax.axis_size("swap")
    screen = tile_slot.shape[0]
    owned = screen // group_count
    arrived, slots, order, start = render(
        samples[0, 0], tile_list, tile_slot, brick_rank, group_count
    )
    parts = composite(
        arrived, order.reshape(-1), start.reshape(-1), slots.reshape(-1), screen, 2 * swap_count
    )
    return finish(parts, swap_count, group_count, owned)[None]


def solution(mesh):
    return jax.shard_map(
        shards,
        mesh=mesh,
        in_specs=(P("swap", "grp", None, None, None), P(), P(), P()),
        out_specs=P("grp", None, None, "swap"),
        check_vma=False,
    )
```

```python
import functools

import jax
import jax.numpy as jnp
from jax import lax
from jax.experimental import pallas as pl
from jax.experimental.pallas import tpu as pltpu
from jax.sharding import PartitionSpec as P

BRICKS = 8
LANES = 128
HALF = 64

EXTINCTION = 0.024
MESH = pl.DeviceIdType.MESH


def halves(shape):
    return lax.broadcasted_iota(jnp.int32, shape, len(shape) - 1) < HALF


def swapped(value):
    return pltpu.roll(value, HALF, value.ndim - 1)


def chip_at(step, chips):
    columns = 8 if chips % 32 == 0 else 2
    rows = chips // columns
    mine = lax.axis_index("grp") // 2
    turn = columns - 1 - (step // rows + step % rows) % columns
    along = ((turn + 1) // 2) * (2 * (turn % 2) - 1)
    x = (mine // columns + step % rows) % rows
    y = (mine % columns + along + columns) % columns
    return x * columns + y


def render_kernel(
    samples_ref,
    tiles_ref,
    tile_slot_ref,
    rank_ref,
    out_ref,
    slots_ref,
    order_ref,
    start_ref,
    levels,
    stage,
    send_sem,
    recv_sem,
    own_sem,
):
    fragments, depth_count, _ = samples_ref.shape
    group_count = out_ref.shape[0]
    chips = group_count // 2
    half = fragments // 2
    early = chips // 8 if chips % 8 == 0 else 1
    me = lax.axis_index("grp")
    slab = lax.axis_index("swap")
    barrier = pltpu.get_barrier_semaphore()

    def greet(step, carry):
        other = (me + step) % group_count
        pl.semaphore_signal(barrier, inc=1, device_id=(other, slab), device_id_type=MESH)
        return carry

    lax.fori_loop(1, group_count, greet, 0)

    def paint(row):
        at = pl.multiple_of(row * LANES, LANES)
        low = halves((fragments, LANES))
        low_half = halves((half, LANES))
        levels[...] = samples_ref[:, :, pl.ds(at, LANES)].astype(jnp.float32)
        passed = jnp.ones((fragments, LANES), jnp.float32)
        red = jnp.zeros((fragments, LANES), jnp.float32)
        green = jnp.zeros((fragments, LANES), jnp.float32)
        for level in range(depth_count):
            value = levels[:, level, :]
            through = jnp.exp(-EXTINCTION * value)
            weight = passed * (1.0 - through)
            rest = 1.0 / (1.0 + value)
            ratio = value * rest
            shade = weight * ratio
            red = red + shade
            green = green + shade * 4.0 * rest
            passed = passed * through
        red_swapped, green_swapped, passed_swapped = swapped(red), swapped(green), swapped(passed)
        stage[2 * row, :fragments, :] = jnp.where(low, red, green_swapped)
        stage[2 * row + 1, :fragments, :] = jnp.where(low, red_swapped, green)
        stage[2 * row, fragments:, :] = jnp.where(low_half, passed[:half], passed_swapped[half:])
        stage[2 * row + 1, fragments:, :] = jnp.where(
            low_half, passed_swapped[:half], passed[half:]
        )

    def sending(target):
        return pltpu.make_async_remote_copy(
            src_ref=stage.at[target],
            dst_ref=out_ref.at[me],
            send_sem=send_sem.at[target],
            recv_sem=recv_sem.at[me],
            device_id=(target, slab),
            device_id_type=MESH,
        )

    def keeping():
        return pltpu.make_async_copy(stage.at[me], out_ref.at[me], own_sem)

    def send(row):
        for side in range(2):
            target = 2 * row + side

            @pl.when(target != me)
            def _():
                sending(target).start()

            @pl.when(target == me)
            def _():
                keeping().start()

    def first(step, carry):
        paint(chip_at(step, chips))
        return carry

    def first_send(step, carry):
        send(chip_at(step, chips))
        return carry

    def later(step, carry):
        row = chip_at(step, chips)
        paint(row)
        send(row)
        return carry

    lax.fori_loop(0, early, first, 0)
    pl.semaphore_wait(barrier, group_count - 1)
    lax.fori_loop(0, early, first_send, 0)
    lax.fori_loop(early, chips, later, 0)

    tiles = tiles_ref[slab]

    def find_slot(tile, slots):
        return jnp.where(tiles == tile, 2 * tile_slot_ref[tile], slots)

    slots = lax.fori_loop(
        0, tile_slot_ref.shape[0], find_slot, jnp.zeros_like(tiles), unroll=8
    )
    pairs = group_count // 2
    slots_ref[...] = jnp.concatenate([slots[:pairs], slots[pairs:]], axis=1)
    place = lax.broadcasted_iota(jnp.int32, order_ref.shape, 0) * order_ref.shape[1]
    place = place + lax.broadcasted_iota(jnp.int32, order_ref.shape, 1)

    def find_brick(brick, order):
        return jnp.where(place == rank_ref[slab, brick], brick, order)

    order = lax.fori_loop(0, rank_ref.shape[1], find_brick, jnp.zeros_like(place), unroll=8)
    per_brick = fragments // BRICKS
    source = order // BRICKS
    upper = (source >= pairs).astype(jnp.int32)
    order_ref[...] = order * (2 * per_brick)
    start_ref[...] = (
        (source - upper * pairs) * (2 * fragments)
        + upper * fragments
        + (order - source * BRICKS) * per_brick
    )

    def finish_one(step, carry):
        other = (me + step) % group_count
        sending(other).wait_send()
        pltpu.make_async_remote_copy(
            src_ref=stage.at[other],
            dst_ref=out_ref.at[other],
            send_sem=send_sem.at[other],
            recv_sem=recv_sem.at[other],
            device_id=(other, slab),
            device_id_type=MESH,
        ).wait_recv()
        return carry

    lax.fori_loop(1, group_count, finish_one, 0)
    keeping().wait()


def render(samples, tile_list, tile_slot, brick_rank, group_count):
    fragments, depth_count, pixels = samples.shape
    rows = fragments + fragments // 2
    bricks = brick_rank.shape[1]
    lanes = min(bricks, LANES)
    return pl.pallas_call(
        render_kernel,
        in_specs=[
            pl.BlockSpec(memory_space=pltpu.VMEM),
            pl.BlockSpec(memory_space=pltpu.VMEM),
            pl.BlockSpec(memory_space=pltpu.SMEM),
            pl.BlockSpec(memory_space=pltpu.SMEM),
        ],
        out_specs=(
            pl.BlockSpec(memory_space=pl.ANY),
            pl.BlockSpec(memory_space=pltpu.VMEM),
            pl.BlockSpec(memory_space=pltpu.VMEM),
            pl.BlockSpec(memory_space=pltpu.VMEM),
        ),
        out_shape=(
            jax.ShapeDtypeStruct((group_count, rows, LANES), jnp.float32),
            jax.ShapeDtypeStruct((group_count // 2, 2 * fragments), jnp.int32),
            jax.ShapeDtypeStruct((bricks // lanes, lanes), jnp.int32),
            jax.ShapeDtypeStruct((bricks // lanes, lanes), jnp.int32),
        ),
        scratch_shapes=[
            pltpu.VMEM((fragments, depth_count, LANES), jnp.float32),
            pltpu.VMEM((group_count, rows, LANES), jnp.float32),
            pltpu.SemaphoreType.DMA((group_count,)),
            pltpu.SemaphoreType.DMA((group_count,)),
            pltpu.SemaphoreType.DMA,
        ],
        compiler_params=pltpu.CompilerParams(collective_id=0, has_side_effects=True),
        cost_estimate=pl.CostEstimate(
            flops=40 * samples.size, bytes_accessed=8 << 20, transcendentals=samples.size
        ),
    )(samples, tile_list, tile_slot, brick_rank)


def composite_kernel(
    order_ref, start_ref, slots_ref, pieces_ref, out_ref, parts, state, *, fragments
):
    rows = fragments * 3 // 2
    sources = pieces_ref.shape[0] // rows
    half = fragments // 2
    per_brick = fragments // BRICKS
    bricks = sources * BRICKS
    clear = state.shape[0] // sources
    low_half = halves((half, LANES))
    odd = lax.broadcasted_iota(jnp.int32, (clear, LANES), 0) & 1
    upper = lax.broadcasted_iota(jnp.int32, (2, LANES), 0) == 0

    def widen(source, carry):
        start = pl.multiple_of(source * rows, 8)
        packed = pieces_ref[pl.ds(start + fragments, half), :]
        turned = swapped(packed)
        at = pl.multiple_of(source * (2 * fragments), 8)
        parts[pl.ds(at, fragments, stride=2), :] = pieces_ref[pl.ds(start, fragments), :]
        parts[pl.ds(at + 1, half, stride=2), :] = jnp.where(low_half, packed, turned)
        parts[pl.ds(at + fragments + 1, half, stride=2), :] = jnp.where(low_half, turned, packed)
        state[pl.ds(pl.multiple_of(source * clear, clear), clear), :] = odd.astype(jnp.float32)
        return carry

    lax.fori_loop(0, sources, widen, 0)

    def fetch(start):
        return tuple(slots_ref[start + i] for i in range(per_brick))

    def brick_step(rank, slots):
        slots_after = fetch(start_ref[jnp.minimum(rank + 1, bricks - 1)])
        at = pl.multiple_of(order_ref[rank], 2 * per_brick)
        held = [state[pl.ds(pl.multiple_of(slot, 2), 2), :] for slot in slots]
        for i in range(per_brick):
            seen = jnp.broadcast_to(held[i][1:], (2, LANES))
            added = seen * parts[pl.ds(at + 2 * i, 2), :]
            state[pl.ds(pl.multiple_of(slots[i], 2), 2), :] = added + jnp.where(
                upper, held[i], 0.0
            )
        return slots_after

    lax.fori_loop(0, bricks, brick_step, fetch(start_ref[0]), unroll=2)
    groups, packed_rows, _ = out_ref.shape
    size = packed_rows * 2 // 3
    low_size = halves((size // 2, LANES))
    for group in range(groups):
        at = group * 2 * size
        out_ref[group, :size, :] = state[pl.ds(at, size, stride=2), :]
        out_ref[group, size:, :] = jnp.where(
            low_size,
            state[pl.ds(at + 1, size // 2, stride=2), :],
            state[pl.ds(at + size + 1, size // 2, stride=2), :],
        )


def composite(pieces, order, start, slots, screen, groups):
    sources, rows, _ = pieces.shape
    fragments = rows * 2 // 3
    size = screen // groups
    return pl.pallas_call(
        functools.partial(composite_kernel, fragments=fragments),
        in_specs=[
            pl.BlockSpec(memory_space=pltpu.SMEM),
            pl.BlockSpec(memory_space=pltpu.SMEM),
            pl.BlockSpec(memory_space=pltpu.SMEM),
            pl.BlockSpec(memory_space=pltpu.VMEM),
        ],
        out_specs=pl.BlockSpec(memory_space=pltpu.VMEM),
        out_shape=jax.ShapeDtypeStruct((groups, size + size // 2, LANES), jnp.float32),
        scratch_shapes=[
            pltpu.VMEM((2 * sources * fragments, LANES), jnp.float32),
            pltpu.VMEM((2 * screen, LANES), jnp.float32),
        ],
    )(order, start, slots, pieces.reshape(sources * rows, LANES))


def finish_kernel(
    part_ref, out_ref, arrived, stage, landed, own_sem, send_sem, recv_sem, out_sem, in_sem, here_sem
):
    packed_rows = part_ref.shape[1]
    slabs = part_ref.shape[0] // 2
    size = packed_rows * 2 // 3
    half = size // 2
    blocks, rows, _ = landed.shape
    owned = rows // 2
    me = lax.axis_index("grp")
    slab = lax.axis_index("swap")
    inside = me // blocks == slab
    barrier = pltpu.get_barrier_semaphore()
    for step in range(1, slabs):
        other = (slab + step) % slabs
        pl.semaphore_signal(barrier, inc=1, device_id=(me, other), device_id_type=MESH)
    for block in range(blocks):
        source = slab * blocks + block

        @pl.when(jnp.logical_not(inside & (source == me)))
        def _():
            pl.semaphore_signal(
                barrier, inc=1, device_id=(source, me // blocks), device_id_type=MESH
            )

    def own(side):
        return pltpu.make_async_copy(
            part_ref.at[2 * slab + side], arrived.at[side, slab], own_sem.at[side]
        )

    own(0).start()
    own(1).start()

    @pl.when(inside)
    def _():
        pl.semaphore_wait(barrier, slabs + blocks - 2)

    @pl.when(jnp.logical_not(inside))
    def _():
        pl.semaphore_wait(barrier, slabs + blocks - 1)

    def across(side, other):
        return pltpu.make_async_remote_copy(
            src_ref=part_ref.at[2 * other + side],
            dst_ref=arrived.at[side, slab],
            send_sem=send_sem.at[side, other],
            recv_sem=recv_sem.at[side, slab],
            device_id=(me, other),
            device_id_type=MESH,
        )

    def from_slab(side, other):
        return pltpu.make_async_remote_copy(
            src_ref=part_ref.at[2 * other + side],
            dst_ref=arrived.at[side, other],
            send_sem=send_sem.at[side, other],
            recv_sem=recv_sem.at[side, other],
            device_id=(me, other),
            device_id_type=MESH,
        )

    for side in range(2):
        for step in range(1, slabs):
            across(side, (slab + slabs - step) % slabs).start()
    low_half = halves((half, LANES))

    def merge(side):
        own(side).wait()
        color = jnp.zeros((size, LANES), jnp.float32)
        passed = [jnp.ones((half, LANES), jnp.float32)] * 2
        for number in range(slabs):

            @pl.when(slab != number)
            def _():
                from_slab(side, number).wait_recv()

            packed = arrived[side, number, size:, :]
            turned = swapped(packed)
            color = color + jnp.concatenate(passed, axis=0) * arrived[side, number, :size, :]
            passed = [
                passed[0] * jnp.where(low_half, packed, turned),
                passed[1] * jnp.where(low_half, turned, packed),
            ]
        return color, jnp.concatenate(passed, axis=0)

    def to_owner(block):
        return pltpu.make_async_remote_copy(
            src_ref=stage.at[block],
            dst_ref=landed.at[me % blocks],
            send_sem=out_sem.at[block],
            recv_sem=in_sem.at[me % blocks],
            device_id=(slab * blocks + block, me // blocks),
            device_id_type=MESH,
        )

    def from_block(block):
        return pltpu.make_async_remote_copy(
            src_ref=stage.at[block],
            dst_ref=landed.at[block],
            send_sem=out_sem.at[block],
            recv_sem=in_sem.at[block],
            device_id=(slab * blocks + block, me // blocks),
            device_id_type=MESH,
        )

    def stay():
        return pltpu.make_async_copy(stage.at[me % blocks], landed.at[me % blocks], here_sem)

    for side in range(2):
        color, passed = merge(side)
        first = side * blocks // 2
        for block in range(first, first + blocks // 2):
            at = (block - first) * owned
            stage[block, :owned, :] = color[at : at + owned]
            stage[block, owned:, :] = passed[at : at + owned]
        for block in range(first, first + blocks // 2):
            here = inside & (slab * blocks + block == me)

            @pl.when(here)
            def _():
                stay().start()

            @pl.when(jnp.logical_not(here))
            def _():
                to_owner(block).start()

    for side in range(2):
        for step in range(1, slabs):
            across(side, (slab + slabs - step) % slabs).wait_send()
    for block in range(blocks):
        here = inside & (slab * blocks + block == me)

        @pl.when(here)
        def _():
            stay().wait()

        @pl.when(jnp.logical_not(here))
        def _():
            to_owner(block).wait_send()
            from_block(block).wait_recv()

    low = halves((owned, LANES))
    for pair in range(blocks // 2):
        color_low, passed_low = landed[2 * pair, :owned, :], landed[2 * pair, owned:, :]
        color_high, passed_high = landed[2 * pair + 1, :owned, :], landed[2 * pair + 1, owned:, :]
        red = jnp.where(low, color_low, swapped(color_high))
        green = jnp.where(low, swapped(color_low), color_high)
        opacity = 1.0 - jnp.where(low, passed_low, passed_high)
        at = pair * LANES
        out_ref[:, 0, at : at + LANES] = red
        out_ref[:, 1, at : at + LANES] = green
        out_ref[:, 2, at : at + LANES] = opacity - red
        out_ref[:, 3, at : at + LANES] = opacity


def finish(parts, slabs, group_count, owned):
    blocks = group_count // slabs
    return pl.pallas_call(
        finish_kernel,
        in_specs=[pl.BlockSpec(memory_space=pltpu.VMEM)],
        out_specs=pl.BlockSpec(memory_space=pltpu.VMEM),
        out_shape=jax.ShapeDtypeStruct((owned, 4, blocks * HALF), jnp.float32),
        scratch_shapes=[
            pltpu.VMEM((2, slabs) + parts.shape[1:], jnp.float32),
            pltpu.VMEM((blocks, 2 * owned, LANES), jnp.float32),
            pltpu.VMEM((blocks, 2 * owned, LANES), jnp.float32),
            pltpu.SemaphoreType.DMA((2,)),
            pltpu.SemaphoreType.DMA((2, slabs)),
            pltpu.SemaphoreType.DMA((2, slabs)),
            pltpu.SemaphoreType.DMA((blocks,)),
            pltpu.SemaphoreType.DMA((blocks,)),
            pltpu.SemaphoreType.DMA,
        ],
        compiler_params=pltpu.CompilerParams(collective_id=1, has_side_effects=True),
    )(parts)


def shards(samples, tile_list, tile_slot, brick_rank):
    group_count = lax.axis_size("grp")
    swap_count = lax.axis_size("swap")
    screen = tile_slot.shape[0]
    owned = screen // group_count
    arrived, slots, order, start = render(
        samples[0, 0], tile_list, tile_slot, brick_rank, group_count
    )
    parts = composite(
        arrived, order.reshape(-1), start.reshape(-1), slots.reshape(-1), screen, 2 * swap_count
    )
    return finish(parts, swap_count, group_count, owned)[None]


def solution(mesh):
    return jax.shard_map(
        shards,
        mesh=mesh,
        in_specs=(P("swap", "grp", None, None, None), P(), P(), P()),
        out_specs=P("grp", None, None, "swap"),
        check_vma=False,
    )
```
